1024 devices in a mesh: grp: 16 (over x, z_lo), dom: 64 (over y, z_hi, core).
Axes of the slice: x: 8, y: 8, z: 8 (z_hi: 4, z_lo: 2; z = z_hi * 2 + z_lo), core: 2. Of those that a mesh axis runs over, the one named last changes fastest.
Arguments:
- pert_fcst: bfloat16 [32, 8, 2, 64, 4096], P('grp', None, None, 'dom'), may hold values from -6 to 6
- control: float32 [32, 8, 256, 1024], P('grp', None, 'dom'), may hold values from -6 to 6
- departures: float32 [8, 2, 256, 1024], P(None, None, 'dom'), may hold values from -6 to 6
- obs_weight: float32 [8, 2, 256, 1024], P(None, None, 'dom'), may hold values from 0.3 to 3
- diff_rate: float32 [8], replicated, may hold values from 0.05 to 0.24
- step_counts: int32 [8], replicated, may hold values from 1 to 4, as said below
Outputs:
- increment: float32 [8, 2, 256, 1024], P(None, None, 'dom')
- gradient: float32 [32, 8, 256, 1024], P('grp', None, 'dom')
The draws below stay inside these ranges and needn't reach their ends.
Inputs may be any that keep to these rules, and one draw needn't show every extreme that they name: `step_counts`: some level has exactly 4 sweeps.
All inputs are finite; a program needn't handle non-finite values.
Results may differ from the reference program's by a relative error of at most 0.0003.
Values may be sent and summed in bfloat16 or wider, within the bound.
A program may use at most 32 MiB of HBM per device.

```python
import math
import jax
import jax.numpy as jnp
from jax import lax

LEV = 8
VAR = 2
NSTEP = 4
LON_DEV = 16
MEMBERS = 32
NLAT = 256
NLON = 1024
N_DOM = 64


def draw_step_counts(key, part):
    counts = jax.random.randint(key, (LEV,), 1, NSTEP + 1, dtype=jnp.int32)
    chosen = jax.random.randint(jax.random.fold_in(key, 7), (), 0, LEV, dtype=jnp.int32)
    return jnp.where(jnp.arange(LEV, dtype=jnp.int32) == chosen, NSTEP, counts).astype(jnp.int32)


def block_levels(key, extent, cuts, smallest, top_value):
    def one(position, shards_of):
        heights = jax.random.uniform(jax.random.fold_in(jax.random.fold_in(key, 6), position), (shards_of,), jnp.float32, smallest / len(cuts), top_value / len(cuts))
        return jnp.repeat(jnp.exp(heights), extent[position] // shards_of).reshape((-1,) + (1,) * (len(extent) - position - 1))

    level = one(*cuts[0])
    for cut in cuts[1:]:
        level = level * one(*cut)
    return level


def normal_values(stream_key, shape, scale, reach, split=(), held_as=jnp.bfloat16):
    gain = block_levels(stream_key, shape, split, -0.22, 0.18) if split else 1.0
    entries = jax.random.normal(stream_key, shape, jnp.float32) * scale * gain
    return jnp.minimum(jnp.maximum(entries, -reach), reach).astype(held_as)


def setup_inputs(seed: int = 0) -> dict:
    key_list = jax.random.split(jax.random.key(seed), 7)
    return {
        "pert_fcst": normal_values(key_list[0], (MEMBERS, LEV, VAR, N_DOM, NLAT * LON_DEV), 1.0, 6.0, ((0, 16), (3, 64))),
        "control": normal_values(key_list[1], (MEMBERS, LEV, NLAT, NLON), 1.0, 6.0, ((0, 16), (2, 64)), jnp.float32),
        "departures": normal_values(key_list[2], (LEV, VAR, NLAT, NLON), 1.0, 6.0, ((2, 64),), jnp.float32),
        "obs_weight": jnp.clip(jnp.exp(math.log(3.0) - 2.3025851 * jax.random.uniform(key_list[3], (LEV, VAR, NLAT, NLON), jnp.float32) ** block_levels(key_list[3], (LEV, VAR, NLAT, NLON), ((2, 64),), -0.2, 0.2)), 0.3, 3.0),
        "diff_rate": jnp.clip(jax.random.uniform(key_list[4], (LEV,), jnp.float32, 0.05, 0.24), 0.05, 0.24),
        "step_counts": draw_step_counts(jax.random.fold_in(key_list[6], 71), 0),
    }


def diffuse(field_now, diff_rate, step_counts):
    for sweep_index in range(NSTEP):
        padded = jnp.pad(field_now, ((0, 0), (1, 1), (0, 0)))
        laplace = padded[:, 2:] + padded[:, :-2] + jnp.roll(field_now, 1, axis=2) + jnp.roll(field_now, -1, axis=2) - 4.0 * field_now
        updated = field_now + diff_rate[:, None, None] * laplace
        field_now = jnp.where((sweep_index < step_counts)[:, None, None], updated, field_now)
    return field_now

def relayout(pert_member):
    blocks = pert_member.reshape(LEV, VAR, N_DOM, NLAT, LON_DEV)
    return blocks.transpose(0, 1, 3, 2, 4).reshape(LEV, VAR, NLAT, NLON)

def reference(pert_fcst, control, departures, obs_weight, diff_rate, step_counts):
    factor = 1.0 / math.sqrt(MEMBERS - 1)

    def add_member(carry_sum, inputs):
        pert_member, control_member = inputs
        localized = diffuse(control_member, diff_rate, step_counts)
        projected = relayout(pert_member).astype(jnp.float32) * localized[:, None]
        return (carry_sum + projected, None)
    start = jnp.zeros((LEV, VAR, NLAT, NLON), jnp.float32)
    summed = lax.scan(add_member, start, (pert_fcst, control))[0]
    increment = summed * factor
    residual = obs_weight * (increment - departures)

    def member_grad(inputs):
        pert_member, control_member = inputs
        adjoint = lax.optimization_barrier(jnp.sum(relayout(pert_member).astype(jnp.float32) * residual, axis=1)) * factor
        return control_member + diffuse(adjoint, diff_rate, step_counts)
    gradient = lax.map(member_grad, (pert_fcst, control))
    return (increment, gradient)
```

```python
import functools
import math

import jax
import jax.numpy as jnp
from jax import lax
from jax.experimental import pallas as pl
from jax.experimental.pallas import tpu as pltpu
from jax.sharding import PartitionSpec as P

NSTEP = 4
MEM = 2
LEV = 8
VAR = 2
ROWS = 4
LON = 1024
LANES = 128
TILES = LON // LANES
SLOT = 16
HALF = LON // 2
NDOM = 64
NGRP = 16
MESH = pl.DeviceIdType.MESH


def lane_iota(shape):
    return lax.broadcasted_iota(jnp.int32, shape, len(shape) - 1)


def remote(src, dst, send_sem, recv_sem, device):
    return pltpu.make_async_remote_copy(
        src_ref=src,
        dst_ref=dst,
        send_sem=send_sem,
        recv_sem=recv_sem,
        device_id=device,
        device_id_type=MESH,
    )


def wait_bytes(ref, sem):
    pltpu.make_async_copy(ref, ref, sem).wait()


def wide(tile):
    return jnp.concatenate([tile] * TILES, axis=1)


def sweeps(src, other, coef, m, emit):
    bufs = (src, other)
    for s in range(NSTEP):
        old, new = bufs[s % 2], bufs[(s + 1) % 2]
        first, last = s + 1, 3 * ROWS - 1 - s
        north = old[m, first - 1]
        here = old[m, first]
        for row in range(first, last):
            south = old[m, row + 1]
            which = 0 if ROWS <= row < 2 * ROWS else (1 if row < ROWS else 2)
            rate = wide(coef[3 * s + which])
            lap = (
                north
                + south
                + pltpu.roll(here, 1, axis=1)
                + pltpu.roll(here, LON - 1, axis=1)
                - 4.0 * here
            )
            value = here + rate * lap
            if s == NSTEP - 1:
                emit(row - ROWS, value)
            else:
                new[m, row] = value
            north, here = here, south


def kernel(
    factor,
    rate_ref,
    steps_ref,
    pert_ref,
    ctl_ref,
    dep_ref,
    wgt_ref,
    inc_ref,
    grad_ref,
    pf,
    packed,
    got,
    pert,
    up_raw,
    dn_raw,
    ext,
    tmp,
    ext2,
    loc,
    coef,
    part,
    red,
    incs,
    a2a_send,
    a2a_recv,
    halo_send,
    halo_recv,
    rs_send,
    rs_recv,
    ag_send,
    ag_recv,
    adj_send,
    adj_recv,
):
    g = lax.axis_index("grp")
    d = lax.axis_index("dom")
    below = lax.rem(d + 1, NDOM)
    above = lax.rem(d + NDOM - 1, NDOM)

    barrier = pltpu.get_barrier_semaphore()

    def greet_dom(k, carry):
        pl.semaphore_signal(
            barrier, inc=1, device_id=(g, lax.rem(d + k, NDOM)), device_id_type=MESH
        )
        return carry

    def greet_grp(k, carry):
        pl.semaphore_signal(
            barrier, inc=1, device_id=(lax.rem(g + k, NGRP), d), device_id_type=MESH
        )
        return carry

    lax.fori_loop(1, NDOM, greet_dom, 0)
    lax.fori_loop(1, NGRP, greet_grp, 0)

    pf[...] = pert_ref[...].astype(jnp.float32)
    low = lane_iota((LEV, LANES)) < 64

    def pack(q, carry):
        firsts, seconds = [], []
        for v in range(VAR):
            a = pf[pl.ds(q * 2 + v, LEV, stride=64), :]
            b = pf[pl.ds(512 + q * 2 + v, LEV, stride=64), :]
            firsts.append(jnp.where(low, a, pltpu.roll(b, 64, axis=1)))
            seconds.append(jnp.where(low, pltpu.roll(a, 64, axis=1), b))
        packed[2 * q] = jnp.concatenate(firsts, axis=0).astype(jnp.bfloat16)
        packed[2 * q + 1] = jnp.concatenate(seconds, axis=0).astype(jnp.bfloat16)
        return carry

    lax.fori_loop(0, NDOM // 2, pack, 0)

    level = lax.broadcasted_iota(jnp.int32, (LEV, LANES), 0)
    rate = jnp.zeros((LEV, LANES), jnp.float32)
    count = jnp.zeros((LEV, LANES), jnp.int32)
    for l in range(LEV):
        rate = jnp.where(level == l, rate_ref[l], rate)
        count = jnp.where(level == l, steps_ref[l], count)
    has_up = jnp.where(d > 0, 1.0, 0.0).astype(jnp.float32)
    has_dn = jnp.where(d < NDOM - 1, 1.0, 0.0).astype(jnp.float32)
    for s in range(NSTEP):
        now = jnp.where(s < count, rate, 0.0)
        coef[3 * s] = now
        coef[3 * s + 1] = now * has_up
        coef[3 * s + 2] = now * has_dn

    pl.semaphore_wait(barrier, NDOM - 1 + NGRP - 1)

    to_below = remote(ctl_ref, up_raw, halo_send.at[0], halo_recv.at[0], (g, below))
    to_above = remote(ctl_ref, dn_raw, halo_send.at[1], halo_recv.at[1], (g, above))
    to_below.start()
    to_above.start()

    def send_tile(k):
        to = lax.rem(d + k, NDOM)
        remote(packed.at[to], got.at[d], a2a_send, a2a_recv, (g, to)).start()

    send_tile(NDOM // 2)

    def send_pair(j, carry):
        send_tile(NDOM // 2 - j)
        send_tile(NDOM // 2 + j)
        return carry

    lax.fori_loop(1, NDOM // 2, send_pair, 0)
    got[d] = packed[d]

    def fill(source, base_row):
        def body(n, carry):
            m, i = n // ROWS, lax.rem(n, ROWS)
            for t in range(TILES):
                ext[m, base_row + i, :, t * LANES : (t + 1) * LANES] = source[
                    pl.ds(m * 256 + t * ROWS + i, LEV, stride=32), :
                ]
            return carry

        lax.fori_loop(0, MEM * ROWS, body, 0)

    def clear(buffer, base_row):
        for m in range(MEM):
            for i in range(ROWS):
                buffer[m, base_row + i] = jnp.zeros((LEV, LON), jnp.float32)

    fill(ctl_ref, ROWS)
    to_below.wait_recv()
    to_above.wait_recv()
    fill(up_raw, 0)
    fill(dn_raw, 2 * ROWS)

    @pl.when(d == 0)
    def _():
        clear(ext, 0)

    @pl.when(d == NDOM - 1)
    def _():
        clear(ext, 2 * ROWS)

    def localize(m, carry):
        def emit(i, value):
            loc[m * ROWS + i] = value

        sweeps(ext, tmp, coef, m, emit)
        return carry

    lax.fori_loop(0, MEM, localize, 0)

    wait_bytes(got.at[pl.ds(0, NDOM - 1)], a2a_recv)
    slot = lane_iota((2 * LEV, LANES)) // SLOT

    def relayout(t, carry):
        tiles = [got[t * TILES + c].astype(jnp.float32) for c in range(TILES)]
        for step in (4, 2, 1):
            high = (slot & step) != 0
            for a in range(TILES):
                if a & step:
                    continue
                x, y = tiles[a], tiles[a + step]
                tiles[a] = jnp.where(high, pltpu.roll(y, step * SLOT, axis=1), x)
                tiles[a + step] = jnp.where(
                    high, y, pltpu.roll(x, LANES - step * SLOT, axis=1)
                )
        for k in range(TILES):
            pert[k, :, pl.ds(pl.multiple_of(t * LANES, LANES), LANES)] = tiles[k]
        return carry

    lax.fori_loop(0, TILES, relayout, 0)

    def share(n, carry):
        i, h = n // 2, lax.rem(n, 2)
        cols = pl.ds(pl.multiple_of(h * HALF, HALF), HALF)
        for v in range(VAR):
            rows = slice(v * LEV, (v + 1) * LEV)
            part[(v * ROWS + i) * 2 + h] = (
                pert[i, rows, cols] * loc[i, :, cols]
                + pert[ROWS + i, rows, cols] * loc[ROWS + i, :, cols]
            )
        return carry

    lax.fori_loop(0, 2 * ROWS, share, 0)

    def scatter(k, carry):
        to = lax.rem(g + k, NGRP)
        remote(part.at[to], red.at[g], rs_send, rs_recv, (to, d)).start()
        return carry

    lax.fori_loop(1, NGRP, scatter, 0)
    red[g] = part[g]
    wait_bytes(red.at[pl.ds(0, NGRP - 1)], rs_recv)
    total = red[0]
    for n in range(1, NGRP):
        total = total + red[n]
    incs[g] = total * factor

    def gather(k, carry):
        to = lax.rem(g + k, NGRP)
        remote(incs.at[g], incs.at[g], ag_send, ag_recv, (to, d)).start()
        return carry

    lax.fori_loop(1, NGRP, gather, 0)
    wait_bytes(incs.at[pl.ds(0, NGRP - 1)], ag_recv)

    def back(i, carry):
        for h in range(2):
            for c in range(TILES // 2):
                t = h * (TILES // 2) + c
                cols = slice(t * LANES, (t + 1) * LANES)
                res = []
                for v in range(VAR):
                    lines = pl.ds(v * 32 + t * ROWS + i, LEV, stride=64)
                    inc = incs[(v * ROWS + i) * 2 + h, :, c * LANES : (c + 1) * LANES]
                    inc_ref[lines, :] = inc
                    res.append(wgt_ref[lines, :] * (inc - dep_ref[lines, :]))
                for m in range(MEM):
                    ext2[m, ROWS + i, :, cols] = (
                        pert[m * ROWS + i, 0:LEV, cols] * res[0]
                        + pert[m * ROWS + i, LEV : 2 * LEV, cols] * res[1]
                    ) * factor
        return carry

    lax.fori_loop(0, ROWS, back, 0)

    def adj_copies(m):
        own = ext2.at[m, pl.ds(ROWS, ROWS)]
        return (
            remote(own, ext2.at[m, pl.ds(0, ROWS)], adj_send.at[m], adj_recv.at[m], (g, below)),
            remote(
                own,
                ext2.at[m, pl.ds(2 * ROWS, ROWS)],
                adj_send.at[2 + m],
                adj_recv.at[2 + m],
                (g, above),
            ),
        )

    copies = [c for m in range(MEM) for c in adj_copies(m)]
    for c in copies:
        c.start()
    for c in copies:
        c.wait_recv()

    @pl.when(d == 0)
    def _():
        clear(ext2, 0)

    @pl.when(d == NDOM - 1)
    def _():
        clear(ext2, 2 * ROWS)

    def gradient(m, carry):
        def emit(i, value):
            for t in range(TILES):
                lines = pl.ds(m * 256 + t * ROWS + i, LEV, stride=32)
                grad_ref[lines, :] = ctl_ref[lines, :] + value[:, t * LANES : (t + 1) * LANES]

        sweeps(ext2, tmp, coef, m, emit)
        return carry

    for c in copies:
        c.wait_send()
    lax.fori_loop(0, MEM, gradient, 0)

    to_below.wait_send()
    to_above.wait_send()
    wait_bytes(packed.at[pl.ds(0, NDOM - 1)], a2a_send)
    wait_bytes(part.at[pl.ds(0, NGRP - 1)], rs_send)
    wait_bytes(incs.at[pl.ds(0, NGRP - 1)], ag_send)


def tiles_of(x):
    a, b, rows, lon = x.shape
    return (
        x.reshape(a, b, rows, lon // LANES, LANES)
        .transpose(0, 1, 3, 2, 4)
        .reshape(a * b * rows * lon // LANES, LANES)
    )


def from_tiles(x, shape):
    a, b, rows, lon = shape
    return (
        x.reshape(a, b, lon // LANES, rows, LANES).transpose(0, 1, 3, 2, 4).reshape(shape)
    )


def per_device(pert_fcst, control, departures, obs_weight, diff_rate, step_counts):
    members = MEM * lax.axis_size("grp")
    factor = 1.0 / math.sqrt(members - 1)
    pert = (
        pert_fcst.reshape(MEM, LEV, VAR, 32, LANES)
        .transpose(0, 1, 3, 2, 4)
        .reshape(MEM * LEV * 32 * VAR, LANES)
    )
    vmem = pl.BlockSpec(memory_space=pltpu.VMEM)
    smem = pl.BlockSpec(memory_space=pltpu.SMEM)
    flat = (MEM * LEV * ROWS * TILES, LANES)
    f32 = jnp.float32
    dma = pltpu.SemaphoreType.DMA
    inc, grad = pl.pallas_call(
        functools.partial(kernel, factor),
        out_shape=(jax.ShapeDtypeStruct(flat, f32), jax.ShapeDtypeStruct(flat, f32)),
        in_specs=[smem, smem, vmem, vmem, vmem, vmem],
        out_specs=(vmem, vmem),
        scratch_shapes=[
            pltpu.VMEM((1024, LANES), f32),
            pltpu.VMEM((NDOM, 16, LANES), jnp.bfloat16),
            pltpu.VMEM((NDOM, 16, LANES), jnp.bfloat16),
            pltpu.VMEM((MEM * ROWS, VAR * LEV, LON), f32),
            pltpu.VMEM(flat, f32),
            pltpu.VMEM(flat, f32),
            pltpu.VMEM((MEM, 3 * ROWS, LEV, LON), f32),
            pltpu.VMEM((MEM, 3 * ROWS, LEV, LON), f32),
            pltpu.VMEM((MEM, 3 * ROWS, LEV, LON), f32),
            pltpu.VMEM((MEM * ROWS, LEV, LON), f32),
            pltpu.VMEM((3 * NSTEP, LEV, LANES), f32),
            pltpu.VMEM((NGRP, LEV, HALF), f32),
            pltpu.VMEM((NGRP, LEV, HALF), f32),
            pltpu.VMEM((NGRP, LEV, HALF), f32),
            dma,
            dma,
            dma((2,)),
            dma((2,)),
            dma,
            dma,
            dma,
            dma,
            dma((4,)),
            dma((4,)),
        ],
        compiler_params=pltpu.CompilerParams(
            collective_id=0, has_side_effects=True, vmem_limit_bytes=48 * 1024 * 1024
        ),
    )(
        diff_rate,
        step_counts,
        pert,
        tiles_of(control),
        tiles_of(departures),
        tiles_of(obs_weight),
    )
    return (from_tiles(inc, (LEV, VAR, ROWS, LON)), from_tiles(grad, (MEM, LEV, ROWS, LON)))


def solution(mesh):
    in_specs = (
        P("grp", None, None, "dom", None),
        P("grp", None, "dom", None),
        P(None, None, "dom", None),
        P(None, None, "dom", None),
        P(),
        P(),
    )
    out_specs = (P(None, None, "dom", None), P("grp", None, "dom", None))
    return jax.shard_map(
        per_device, mesh=mesh, in_specs=in_specs, out_specs=out_specs, check_vma=False
    )
```

```python
import functools
import math

import jax
import jax.numpy as jnp
from jax import lax
from jax.experimental import pallas as pl
from jax.experimental.pallas import tpu as pltpu
from jax.sharding import PartitionSpec as P

NSTEP = 4
MEM = 2
LEV = 8
VAR = 2
ROWS = 4
LON = 1024
LANES = 128
TILES = LON // LANES
SLOT = 16
HALF = LON // 2
NDOM = 64
NGRP = 16
MESH = pl.DeviceIdType.MESH
FAR_FIRST_8 = (4, 3, 5, 2, 6, 1, 7)
FAR_FIRST_16 = (8, 7, 9, 6, 10, 5, 11, 4, 12, 3, 13, 2, 14, 1, 15)


def lane_iota(shape):
    return lax.broadcasted_iota(jnp.int32, shape, len(shape) - 1)


def remote(src, dst, send_sem, recv_sem, device):
    return pltpu.make_async_remote_copy(
        src_ref=src,
        dst_ref=dst,
        send_sem=send_sem,
        recv_sem=recv_sem,
        device_id=device,
        device_id_type=MESH,
    )


def wait_bytes(ref, sem):
    pltpu.make_async_copy(ref, ref, sem).wait()


def wide(tile):
    return jnp.concatenate([tile] * TILES, axis=1)


def sweeps(src, other, coef, m, emit):
    bufs = (src, other)
    for s in range(NSTEP):
        old, new = bufs[s % 2], bufs[(s + 1) % 2]
        first, last = s + 1, 3 * ROWS - 1 - s
        north = old[m, first - 1]
        here = old[m, first]
        for row in range(first, last):
            south = old[m, row + 1]
            which = 0 if ROWS <= row < 2 * ROWS else (1 if row < ROWS else 2)
            rate = wide(coef[3 * s + which])
            lap = (
                north
                + south
                + pltpu.roll(here, 1, axis=1)
                + pltpu.roll(here, LON - 1, axis=1)
                - 4.0 * here
            )
            value = here + rate * lap
            if s == NSTEP - 1:
                emit(row - ROWS, value)
            else:
                new[m, row] = value
            north, here = here, south


def kernel(
    factor,
    rate_hbm,
    steps_hbm,
    pert_hbm,
    ctl_hbm,
    dep_hbm,
    wgt_hbm,
    inc_ref,
    grad_ref,
    rate_ref,
    steps_ref,
    pert_ref,
    ctl_ref,
    dep_ref,
    wgt_ref,
    pf,
    packed,
    mid,
    got,
    pert,
    up_raw,
    dn_raw,
    ext,
    tmp,
    ext2,
    loc,
    coef,
    part,
    red,
    incs,
    load_sem,
    y_send,
    y_recv,
    z_send,
    z_recv,
    halo_send,
    halo_recv,
    rs_send,
    rs_recv,
    ag_send,
    ag_recv,
    adj_send,
    adj_recv,
):
    loads = [
        pltpu.make_async_copy(src, dst, load_sem.at[n])
        for n, (src, dst) in enumerate(
            (
                (pert_hbm, pert_ref),
                (ctl_hbm, ctl_ref),
                (dep_hbm, dep_ref),
                (wgt_hbm, wgt_ref),
                (rate_hbm, rate_ref),
                (steps_hbm, steps_ref),
            )
        )
    ]
    for load in loads:
        load.start()

    g = lax.axis_index("grp")
    d = lax.axis_index("dom")
    y, c = d // TILES, lax.rem(d, TILES)
    below = lax.rem(d + 1, NDOM)
    above = lax.rem(d + NDOM - 1, NDOM)

    barrier = pltpu.get_barrier_semaphore()

    def greet(to):
        pl.semaphore_signal(barrier, inc=1, device_id=to, device_id_type=MESH)

    def y_mate(k):
        return lax.rem(y + k, TILES)

    def z_mate(k):
        return lax.rem(c + k, TILES)

    for k in FAR_FIRST_8:
        greet((g, y_mate(k) * TILES + c))
        greet((g, y * TILES + z_mate(k)))
    for k in FAR_FIRST_16:
        greet((lax.rem(g + k, NGRP), d))

    @pl.when(c == TILES - 1)
    def _():
        greet((g, below))

    @pl.when(c == 0)
    def _():
        greet((g, above))

    loads[0].wait()
    pf[...] = pert_ref[...].astype(jnp.float32)
    low = lane_iota((LEV, LANES)) < 64
    for v in range(VAR):

        def pack(q, carry):
            a = pf[pl.ds(q * 2 + v, LEV, stride=64), :]
            b = pf[pl.ds(512 + q * 2 + v, LEV, stride=64), :]
            first = jnp.where(low, a, pltpu.roll(b, 64, axis=1))
            second = jnp.where(low, pltpu.roll(a, 64, axis=1), b)
            to_y, to_c = q // 4, 2 * lax.rem(q, 4)
            packed[v, to_y, to_c] = first.astype(jnp.bfloat16)
            packed[v, to_y, to_c + 1] = second.astype(jnp.bfloat16)
            return carry

        lax.fori_loop(0, NDOM // 2, pack, 0, unroll=4)

    loads[1].wait()
    ends = c // (TILES - 1) + (TILES - 1 - c) // (TILES - 1)
    pl.semaphore_wait(barrier, 2 * (TILES - 1) + NGRP - 1 + ends)

    def send_y(v):
        for k in FAR_FIRST_8:
            to = y_mate(k)
            remote(
                packed.at[v, to], mid.at[v, y], y_send.at[v], y_recv.at[v], (g, to * TILES + c)
            ).start()

    def send_z(v):
        wait_bytes(mid.at[v, pl.ds(0, TILES - 1)], y_recv.at[v])
        for k in FAR_FIRST_8:
            to = z_mate(k)
            remote(
                mid.at[v, :, to],
                got.at[v, :, c],
                z_send.at[v],
                z_recv.at[v],
                (g, y * TILES + to),
            ).start()
        got[v, :, c] = mid[v, :, c]

    send_y(0)
    to_below = remote(ctl_ref, up_raw, halo_send.at[0], halo_recv.at[0], (g, below))
    to_above = remote(ctl_ref, dn_raw, halo_send.at[1], halo_recv.at[1], (g, above))
    to_below.start()
    to_above.start()
    send_y(1)
    for v in range(VAR):
        mid[v, y] = packed[v, y]

    loads[4].wait()
    loads[5].wait()

    level = lax.broadcasted_iota(jnp.int32, (LEV, LANES), 0)
    rate = jnp.zeros((LEV, LANES), jnp.float32)
    count = jnp.zeros((LEV, LANES), jnp.int32)
    for l in range(LEV):
        rate = jnp.where(level == l, rate_ref[l], rate)
        count = jnp.where(level == l, steps_ref[l], count)
    has_up = jnp.where(d > 0, 1.0, 0.0).astype(jnp.float32)
    has_dn = jnp.where(d < NDOM - 1, 1.0, 0.0).astype(jnp.float32)
    for s in range(NSTEP):
        now = jnp.where(s < count, rate, 0.0)
        coef[3 * s] = now
        coef[3 * s + 1] = now * has_up
        coef[3 * s + 2] = now * has_dn

    def fill(source, base_row):
        def body(n, carry):
            m, i = n // ROWS, lax.rem(n, ROWS)
            for t in range(TILES):
                ext[m, base_row + i, :, t * LANES : (t + 1) * LANES] = source[
                    pl.ds(m * 256 + t * ROWS + i, LEV, stride=32), :
                ]
            return carry

        lax.fori_loop(0, MEM * ROWS, body, 0)

    def clear(buffer, base_row):
        for m in range(MEM):
            for i in range(ROWS):
                buffer[m, base_row + i] = jnp.zeros((LEV, LON), jnp.float32)

    fill(ctl_ref, ROWS)
    send_z(0)
    send_z(1)

    to_below.wait_recv()
    fill(up_raw, 0)
    to_above.wait_recv()
    fill(dn_raw, 2 * ROWS)

    @pl.when(d == 0)
    def _():
        clear(ext, 0)

    @pl.when(d == NDOM - 1)
    def _():
        clear(ext, 2 * ROWS)

    def localize(m, carry):
        def emit(i, value):
            loc[m * ROWS + i] = value

        sweeps(ext, tmp, coef, m, emit)
        return carry

    lax.fori_loop(0, MEM, localize, 0)

    slot = lane_iota((LEV, LANES)) // SLOT
    masks = {step: (slot & step) != 0 for step in (4, 2, 1)}

    for v in range(VAR):
        wait_bytes(got.at[v, pl.ds(0, TILES - 1)], z_recv.at[v])

        def relayout(t, carry):
            tiles = [got[v, t, n].astype(jnp.float32) for n in range(TILES)]
            for step in (4, 2, 1):
                high = masks[step]
                for a in range(TILES):
                    if a & step:
                        continue
                    p, q = tiles[a], tiles[a + step]
                    tiles[a] = jnp.where(high, pltpu.roll(q, step * SLOT, axis=1), p)
                    tiles[a + step] = jnp.where(
                        high, q, pltpu.roll(p, LANES - step * SLOT, axis=1)
                    )
            for k in range(TILES):
                pert[v, t, k] = tiles[k]
            cols = pl.ds(pl.multiple_of(t * LANES, LANES), LANES)
            for i in range(ROWS):
                part[2 * v + t // 4, 4 * i + lax.rem(t, 4)] = (
                    tiles[i] * loc[i, :, cols] + tiles[ROWS + i] * loc[ROWS + i, :, cols]
                )
            return carry

        lax.fori_loop(0, TILES, relayout, 0, unroll=2)
        for q in (2 * v, 2 * v + 1):
            for k in FAR_FIRST_16:
                to = lax.rem(g + k, NGRP)
                remote(
                    part.at[q, to], red.at[q, g], rs_send.at[q], rs_recv.at[q], (to, d)
                ).start()
            red[q, g] = part[q, g]

    for q in range(2 * VAR):
        wait_bytes(red.at[q, pl.ds(0, NGRP - 1)], rs_recv.at[q])
        total = red[q, 0]
        for n in range(1, NGRP):
            total = total + red[q, n]
        incs[q, g] = total * factor
        for k in FAR_FIRST_16:
            remote(
                incs.at[q, g],
                incs.at[q, g],
                ag_send.at[q],
                ag_recv.at[q],
                (lax.rem(g + k, NGRP), d),
            ).start()

    loads[2].wait()
    loads[3].wait()
    copies = []
    for h in range(2):
        for v in range(VAR):
            wait_bytes(incs.at[2 * v + h, pl.ds(0, NGRP - 1)], ag_recv.at[2 * v + h])

        def back(i, carry):
            for n in range(TILES // 2):
                t = h * (TILES // 2) + n
                cols = slice(t * LANES, (t + 1) * LANES)
                res = []
                for v in range(VAR):
                    lines = pl.ds(v * 32 + t * ROWS + i, LEV, stride=64)
                    inc = incs[2 * v + h, 4 * i + n]
                    inc_ref[lines, :] = inc
                    res.append(wgt_ref[lines, :] * (inc - dep_ref[lines, :]))
                for m in range(MEM):
                    ext2[m, ROWS + i, :, cols] = (
                        pert[0, t, m * ROWS + i] * res[0] + pert[1, t, m * ROWS + i] * res[1]
                    ) * factor
            return carry

        lax.fori_loop(0, ROWS, back, 0)
        cols = pl.ds(h * HALF, HALF)
        own = ext2.at[:, pl.ds(ROWS, ROWS), :, cols]
        for n, (row, to) in enumerate(((0, below), (2 * ROWS, above))):
            copies.append(
                remote(
                    own,
                    ext2.at[:, pl.ds(row, ROWS), :, cols],
                    adj_send.at[2 * h + n],
                    adj_recv.at[2 * h + n],
                    (g, to),
                )
            )
            copies[-1].start()

    to_below.wait_send()
    to_above.wait_send()
    for v in range(VAR):
        wait_bytes(packed.at[v, pl.ds(0, TILES - 1)], y_send.at[v])
        wait_bytes(mid.at[v, pl.ds(0, TILES - 1)], z_send.at[v])
    for q in range(2 * VAR):
        wait_bytes(part.at[q, pl.ds(0, NGRP - 1)], rs_send.at[q])
        wait_bytes(incs.at[q, pl.ds(0, NGRP - 1)], ag_send.at[q])
    for copy in copies:
        copy.wait()

    @pl.when(d == 0)
    def _():
        clear(ext2, 0)

    @pl.when(d == NDOM - 1)
    def _():
        clear(ext2, 2 * ROWS)

    def gradient(m, carry):
        def emit(i, value):
            for t in range(TILES):
                lines = pl.ds(m * 256 + t * ROWS + i, LEV, stride=32)
                grad_ref[lines, :] = ctl_ref[lines, :] + value[:, t * LANES : (t + 1) * LANES]

        sweeps(ext2, tmp, coef, m, emit)
        return carry

    lax.fori_loop(0, MEM, gradient, 0)


def tiles_of(x):
    a, b, rows, lon = x.shape
    return (
        x.reshape(a, b, rows, lon // LANES, LANES)
        .transpose(0, 1, 3, 2, 4)
        .reshape(a * b * rows * lon // LANES, LANES)
    )


def from_tiles(x, shape):
    a, b, rows, lon = shape
    return (
        x.reshape(a, b, lon // LANES, rows, LANES).transpose(0, 1, 3, 2, 4).reshape(shape)
    )


def pin(x):
    return pltpu.with_memory_space_constraint(x, pltpu.HBM)


def per_device(pert_fcst, control, departures, obs_weight, diff_rate, step_counts):
    members = MEM * lax.axis_size("grp")
    factor = 1.0 / math.sqrt(members - 1)
    pert = (
        pert_fcst.reshape(MEM, LEV, VAR, 32, LANES)
        .transpose(0, 1, 3, 2, 4)
        .reshape(MEM * LEV * 32 * VAR, LANES)
    )
    vmem = pl.BlockSpec(memory_space=pltpu.VMEM)
    flat = (MEM * LEV * ROWS * TILES, LANES)
    f32, bf16 = jnp.float32, jnp.bfloat16
    hbm = pl.BlockSpec(memory_space=pltpu.HBM)
    dma = pltpu.SemaphoreType.DMA
    inc, grad = pl.pallas_call(
        functools.partial(kernel, factor),
        out_shape=(jax.ShapeDtypeStruct(flat, f32), jax.ShapeDtypeStruct(flat, f32)),
        in_specs=[hbm] * 6,
        out_specs=(vmem, vmem),
        scratch_shapes=[
            pltpu.SMEM((LEV,), f32),
            pltpu.SMEM((LEV,), jnp.int32),
            pltpu.VMEM((1024, LANES), bf16),
            pltpu.VMEM(flat, f32),
            pltpu.VMEM(flat, f32),
            pltpu.VMEM(flat, f32),
            pltpu.VMEM((1024, LANES), f32),
            pltpu.VMEM((VAR, TILES, TILES, LEV, LANES), bf16),
            pltpu.VMEM((VAR, TILES, TILES, LEV, LANES), bf16),
            pltpu.VMEM((VAR, TILES, TILES, LEV, LANES), bf16),
            pltpu.VMEM((VAR, TILES, MEM * ROWS, LEV, LANES), f32),
            pltpu.VMEM(flat, f32),
            pltpu.VMEM(flat, f32),
            pltpu.VMEM((MEM, 3 * ROWS, LEV, LON), f32),
            pltpu.VMEM((MEM, 3 * ROWS, LEV, LON), f32),
            pltpu.VMEM((MEM, 3 * ROWS, LEV, LON), f32),
            pltpu.VMEM((MEM * ROWS, LEV, LON), f32),
            pltpu.VMEM((3 * NSTEP, LEV, LANES), f32),
            pltpu.VMEM((2 * VAR, NGRP, LEV, LANES), f32),
            pltpu.VMEM((2 * VAR, NGRP, LEV, LANES), f32),
            pltpu.VMEM((2 * VAR, NGRP, LEV, LANES), f32),
            dma((6,)),
            dma((2,)),
            dma((2,)),
            dma((2,)),
            dma((2,)),
            dma((2,)),
            dma((2,)),
            dma((4,)),
            dma((4,)),
            dma((4,)),
            dma((4,)),
            dma((4,)),
            dma((4,)),
        ],
        compiler_params=pltpu.CompilerParams(
            collective_id=0, has_side_effects=True, vmem_limit_bytes=48 * 1024 * 1024
        ),
    )(
        pin(diff_rate),
        pin(step_counts),
        pin(pert),
        pin(tiles_of(control)),
        pin(tiles_of(departures)),
        pin(tiles_of(obs_weight)),
    )
    return (from_tiles(inc, (LEV, VAR, ROWS, LON)), from_tiles(grad, (MEM, LEV, ROWS, LON)))


def solution(mesh):
    in_specs = (
        P("grp", None, None, "dom", None),
        P("grp", None, "dom", None),
        P(None, None, "dom", None),
        P(None, None, "dom", None),
        P(),
        P(),
    )
    out_specs = (P(None, None, "dom", None), P("grp", None, "dom", None))
    return jax.shard_map(
        per_device, mesh=mesh, in_specs=in_specs, out_specs=out_specs, check_vma=False
    )
```

```python
import functools
import math

import jax
import jax.numpy as jnp
from jax import lax
from jax.experimental import pallas as pl
from jax.experimental.pallas import tpu as pltpu
from jax.sharding import PartitionSpec as P

NSTEP = 4
MEM = 2
LEV = 8
VAR = 2
ROWS = 4
LON = 1024
LANES = 128
TILES = LON // LANES
SLOT = 16
HALF = LON // 2
NDOM = 64
NGRP = 16
MESH = pl.DeviceIdType.MESH
FAR_FIRST_8 = (4, 3, 5, 2, 6, 1, 7)
FAR_FIRST_16 = (8, 7, 9, 6, 10, 5, 11, 4, 12, 3, 13, 2, 14, 1, 15)


def lane_iota(shape):
    return lax.broadcasted_iota(jnp.int32, shape, len(shape) - 1)


def remote(src, dst, send_sem, recv_sem, device):
    return pltpu.make_async_remote_copy(
        src_ref=src,
        dst_ref=dst,
        send_sem=send_sem,
        recv_sem=recv_sem,
        device_id=device,
        device_id_type=MESH,
    )


def wait_bytes(ref, sem):
    pltpu.make_async_copy(ref, ref, sem).wait()


def wide(tile):
    return jnp.concatenate([tile] * TILES, axis=1)


def sweeps(src, other, coef, m, emit):
    bufs = (src, other)
    for s in range(NSTEP):
        old, new = bufs[s % 2], bufs[(s + 1) % 2]
        first, last = s + 1, 3 * ROWS - 1 - s
        north = old[m, first - 1]
        here = old[m, first]
        for row in range(first, last):
            south = old[m, row + 1]
            which = 0 if ROWS <= row < 2 * ROWS else (1 if row < ROWS else 2)
            rate = wide(coef[3 * s + which])
            lap = (
                north
                + south
                + pltpu.roll(here, 1, axis=1)
                + pltpu.roll(here, LON - 1, axis=1)
                - 4.0 * here
            )
            value = here + rate * lap
            if s == NSTEP - 1:
                emit(row - ROWS, value)
            else:
                new[m, row] = value
            north, here = here, south


def kernel(
    factor,
    rate_hbm,
    steps_hbm,
    pert_hbm,
    ctl_hbm,
    dep_hbm,
    wgt_hbm,
    inc_ref,
    grad_ref,
    rate_ref,
    steps_ref,
    pert_ref,
    ctl_ref,
    dep_ref,
    wgt_ref,
    pf,
    packed,
    mid,
    got,
    pert,
    up_raw,
    dn_raw,
    ext,
    tmp,
    ext2,
    loc,
    coef,
    part,
    red,
    incs,
    load_sem,
    one_send,
    one_recv,
    two_send,
    two_recv,
    halo_send,
    halo_recv,
    rs_send,
    rs_recv,
    ag_send,
    ag_recv,
    adj_send,
    adj_recv,
):
    loads = [
        pltpu.make_async_copy(src, dst, load_sem.at[n])
        for n, (src, dst) in enumerate(
            (
                (pert_hbm, pert_ref),
                (ctl_hbm, ctl_ref),
                (dep_hbm, dep_ref),
                (wgt_hbm, wgt_ref),
                (rate_hbm, rate_ref),
                (steps_hbm, steps_ref),
            )
        )
    ]
    for load in loads:
        load.start()

    g = lax.axis_index("grp")
    d = lax.axis_index("dom")
    y, c = d // TILES, lax.rem(d, TILES)
    below = lax.rem(d + 1, NDOM)
    above = lax.rem(d + NDOM - 1, NDOM)

    barrier = pltpu.get_barrier_semaphore()

    def greet(to):
        pl.semaphore_signal(barrier, inc=1, device_id=to, device_id_type=MESH)

    def y_mate(k):
        return lax.rem(y + k, TILES)

    def z_mate(k):
        return lax.rem(c + k, TILES)

    for k in FAR_FIRST_8:
        greet((g, y_mate(k) * TILES + c))
        greet((g, y * TILES + z_mate(k)))
    for k in FAR_FIRST_16:
        greet((lax.rem(g + k, NGRP), d))

    @pl.when(c == TILES - 1)
    def _():
        greet((g, below))

    @pl.when(c == 0)
    def _():
        greet((g, above))

    loads[0].wait()
    pf[...] = pert_ref[...].astype(jnp.float32)
    low = lane_iota((LEV, LANES)) < 64
    for v in range(VAR):

        def pack(q, carry):
            a = pf[pl.ds(q * 2 + v, LEV, stride=64), :]
            b = pf[pl.ds(512 + q * 2 + v, LEV, stride=64), :]
            first = jnp.where(low, a, pltpu.roll(b, 64, axis=1))
            second = jnp.where(low, pltpu.roll(a, 64, axis=1), b)
            to_y, to_c = q // 4, 2 * lax.rem(q, 4)
            packed[v, to_y, to_c] = first.astype(jnp.bfloat16)
            packed[v, to_y, to_c + 1] = second.astype(jnp.bfloat16)
            return carry

        lax.fori_loop(0, NDOM // 2, pack, 0, unroll=4)

    loads[1].wait()
    ends = c // (TILES - 1) + (TILES - 1 - c) // (TILES - 1)
    pl.semaphore_wait(barrier, 2 * (TILES - 1) + NGRP - 1 + ends)

    def first_stage(v, k):
        if v == 0:
            to = y_mate(k)
            src, dst, device = packed.at[v, to], mid.at[v, y], (g, to * TILES + c)
        else:
            to = z_mate(k)
            src, dst, device = packed.at[v, :, to], mid.at[v, :, c], (g, y * TILES + to)
        remote(src, dst, one_send.at[v], one_recv.at[v], device).start()

    def second_stage(v, k):
        if v == 0:
            to = z_mate(k)
            src, dst, device = mid.at[v, :, to], got.at[v, :, c], (g, y * TILES + to)
        else:
            to = y_mate(k)
            src, dst, device = mid.at[v, to], got.at[v, y], (g, to * TILES + c)
        remote(src, dst, two_send.at[v], two_recv.at[v], device).start()

    def forward(v):
        wait_bytes(mid.at[v, pl.ds(0, TILES - 1)], one_recv.at[v])
        for k in FAR_FIRST_8:
            second_stage(v, k)
        if v == 0:
            got[v, :, c] = mid[v, :, c]
        else:
            got[v, y] = mid[v, y]

    for k in FAR_FIRST_8:
        for v in range(VAR):
            first_stage(v, k)
    to_below = remote(ctl_ref, up_raw, halo_send.at[0], halo_recv.at[0], (g, below))
    to_above = remote(ctl_ref, dn_raw, halo_send.at[1], halo_recv.at[1], (g, above))
    to_below.start()
    to_above.start()
    mid[0, y] = packed[0, y]
    mid[1, :, c] = packed[1, :, c]
    loads[4].wait()
    loads[5].wait()

    level = lax.broadcasted_iota(jnp.int32, (LEV, LANES), 0)
    rate = jnp.zeros((LEV, LANES), jnp.float32)
    count = jnp.zeros((LEV, LANES), jnp.int32)
    for l in range(LEV):
        rate = jnp.where(level == l, rate_ref[l], rate)
        count = jnp.where(level == l, steps_ref[l], count)
    has_up = jnp.where(d > 0, 1.0, 0.0).astype(jnp.float32)
    has_dn = jnp.where(d < NDOM - 1, 1.0, 0.0).astype(jnp.float32)
    for s in range(NSTEP):
        now = jnp.where(s < count, rate, 0.0)
        coef[3 * s] = now
        coef[3 * s + 1] = now * has_up
        coef[3 * s + 2] = now * has_dn

    def fill(source, base_row):
        def body(n, carry):
            m, i = n // ROWS, lax.rem(n, ROWS)
            for t in range(TILES):
                ext[m, base_row + i, :, t * LANES : (t + 1) * LANES] = source[
                    pl.ds(m * 256 + t * ROWS + i, LEV, stride=32), :
                ]
            return carry

        lax.fori_loop(0, MEM * ROWS, body, 0)

    def clear(buffer, base_row):
        for m in range(MEM):
            for i in range(ROWS):
                buffer[m, base_row + i] = jnp.zeros((LEV, LON), jnp.float32)

    fill(ctl_ref, ROWS)
    forward(0)
    forward(1)

    to_below.wait_recv()
    fill(up_raw, 0)
    to_above.wait_recv()
    fill(dn_raw, 2 * ROWS)

    @pl.when(d == 0)
    def _():
        clear(ext, 0)

    @pl.when(d == NDOM - 1)
    def _():
        clear(ext, 2 * ROWS)

    def localize(m, carry):
        def emit(i, value):
            loc[m * ROWS + i] = value

        sweeps(ext, tmp, coef, m, emit)
        return carry

    lax.fori_loop(0, MEM, localize, 0)

    slot = lane_iota((LEV, LANES)) // SLOT
    masks = {step: (slot & step) != 0 for step in (4, 2, 1)}

    for v in range(VAR):
        wait_bytes(got.at[v, pl.ds(0, TILES - 1)], two_recv.at[v])

        def relayout(t, carry):
            tiles = [got[v, t, n].astype(jnp.float32) for n in range(TILES)]
            for step in (4, 2, 1):
                high = masks[step]
                for a in range(TILES):
                    if a & step:
                        continue
                    p, q = tiles[a], tiles[a + step]
                    tiles[a] = jnp.where(high, pltpu.roll(q, step * SLOT, axis=1), p)
                    tiles[a + step] = jnp.where(
                        high, q, pltpu.roll(p, LANES - step * SLOT, axis=1)
                    )
            for k in range(TILES):
                pert[v, t, k] = tiles[k]
            cols = pl.ds(pl.multiple_of(t * LANES, LANES), LANES)
            for i in range(ROWS):
                part[2 * v + t // 4, 4 * i + lax.rem(t, 4)] = (
                    tiles[i] * loc[i, :, cols] + tiles[ROWS + i] * loc[ROWS + i, :, cols]
                )
            return carry

        lax.fori_loop(0, TILES, relayout, 0, unroll=2)
        for q in (2 * v, 2 * v + 1):
            for k in FAR_FIRST_16:
                to = lax.rem(g + k, NGRP)
                remote(
                    part.at[q, to], red.at[q, g], rs_send.at[q], rs_recv.at[q], (to, d)
                ).start()
            red[q, g] = part[q, g]

    for q in range(2 * VAR):
        wait_bytes(red.at[q, pl.ds(0, NGRP - 1)], rs_recv.at[q])
        total = red[q, 0]
        for n in range(1, NGRP):
            total = total + red[q, n]
        incs[q, g] = total * factor
        for k in FAR_FIRST_16:
            remote(
                incs.at[q, g],
                incs.at[q, g],
                ag_send.at[q],
                ag_recv.at[q],
                (lax.rem(g + k, NGRP), d),
            ).start()

    loads[2].wait()
    loads[3].wait()
    copies = []
    for h in range(2):
        for v in range(VAR):
            wait_bytes(incs.at[2 * v + h, pl.ds(0, NGRP - 1)], ag_recv.at[2 * v + h])

        def back(i, carry):
            for n in range(TILES // 2):
                t = h * (TILES // 2) + n
                cols = slice(t * LANES, (t + 1) * LANES)
                res = []
                for v in range(VAR):
                    lines = pl.ds(v * 32 + t * ROWS + i, LEV, stride=64)
                    inc = incs[2 * v + h, 4 * i + n]
                    inc_ref[lines, :] = inc
                    res.append(wgt_ref[lines, :] * (inc - dep_ref[lines, :]))
                for m in range(MEM):
                    ext2[m, ROWS + i, :, cols] = (
                        pert[0, t, m * ROWS + i] * res[0] + pert[1, t, m * ROWS + i] * res[1]
                    ) * factor
            return carry

        lax.fori_loop(0, ROWS, back, 0)
        cols = pl.ds(h * HALF, HALF)
        own = ext2.at[:, pl.ds(ROWS, ROWS), :, cols]
        for n, (row, to) in enumerate(((0, below), (2 * ROWS, above))):
            copies.append(
                remote(
                    own,
                    ext2.at[:, pl.ds(row, ROWS), :, cols],
                    adj_send.at[2 * h + n],
                    adj_recv.at[2 * h + n],
                    (g, to),
                )
            )
            copies[-1].start()

    to_below.wait_send()
    to_above.wait_send()
    for v in range(VAR):
        wait_bytes(packed.at[v, pl.ds(0, TILES - 1)], one_send.at[v])
        wait_bytes(mid.at[v, pl.ds(0, TILES - 1)], two_send.at[v])
    for q in range(2 * VAR):
        wait_bytes(part.at[q, pl.ds(0, NGRP - 1)], rs_send.at[q])
        wait_bytes(incs.at[q, pl.ds(0, NGRP - 1)], ag_send.at[q])
    for copy in copies:
        copy.wait()

    @pl.when(d == 0)
    def _():
        clear(ext2, 0)

    @pl.when(d == NDOM - 1)
    def _():
        clear(ext2, 2 * ROWS)

    def gradient(m, carry):
        def emit(i, value):
            for t in range(TILES):
                lines = pl.ds(m * 256 + t * ROWS + i, LEV, stride=32)
                grad_ref[lines, :] = ctl_ref[lines, :] + value[:, t * LANES : (t + 1) * LANES]

        sweeps(ext2, tmp, coef, m, emit)
        return carry

    lax.fori_loop(0, MEM, gradient, 0)


def tiles_of(x):
    a, b, rows, lon = x.shape
    return (
        x.reshape(a, b, rows, lon // LANES, LANES)
        .transpose(0, 1, 3, 2, 4)
        .reshape(a * b * rows * lon // LANES, LANES)
    )


def from_tiles(x, shape):
    a, b, rows, lon = shape
    return (
        x.reshape(a, b, lon // LANES, rows, LANES).transpose(0, 1, 3, 2, 4).reshape(shape)
    )


def pin(x):
    return pltpu.with_memory_space_constraint(x, pltpu.HBM)


def per_device(pert_fcst, control, departures, obs_weight, diff_rate, step_counts):
    members = MEM * lax.axis_size("grp")
    factor = 1.0 / math.sqrt(members - 1)
    pert = (
        pert_fcst.reshape(MEM, LEV, VAR, 32, LANES)
        .transpose(0, 1, 3, 2, 4)
        .reshape(MEM * LEV * 32 * VAR, LANES)
    )
    vmem = pl.BlockSpec(memory_space=pltpu.VMEM)
    flat = (MEM * LEV * ROWS * TILES, LANES)
    f32, bf16 = jnp.float32, jnp.bfloat16
    hbm = pl.BlockSpec(memory_space=pltpu.HBM)
    dma = pltpu.SemaphoreType.DMA
    inc, grad = pl.pallas_call(
        functools.partial(kernel, factor),
        out_shape=(jax.ShapeDtypeStruct(flat, f32), jax.ShapeDtypeStruct(flat, f32)),
        in_specs=[hbm] * 6,
        out_specs=(vmem, vmem),
        scratch_shapes=[
            pltpu.SMEM((LEV,), f32),
            pltpu.SMEM((LEV,), jnp.int32),
            pltpu.VMEM((1024, LANES), bf16),
            pltpu.VMEM(flat, f32),
            pltpu.VMEM(flat, f32),
            pltpu.VMEM(flat, f32),
            pltpu.VMEM((1024, LANES), f32),
            pltpu.VMEM((VAR, TILES, TILES, LEV, LANES), bf16),
            pltpu.VMEM((VAR, TILES, TILES, LEV, LANES), bf16),
            pltpu.VMEM((VAR, TILES, TILES, LEV, LANES), bf16),
            pltpu.VMEM((VAR, TILES, MEM * ROWS, LEV, LANES), f32),
            pltpu.VMEM(flat, f32),
            pltpu.VMEM(flat, f32),
            pltpu.VMEM((MEM, 3 * ROWS, LEV, LON), f32),
            pltpu.VMEM((MEM, 3 * ROWS, LEV, LON), f32),
            pltpu.VMEM((MEM, 3 * ROWS, LEV, LON), f32),
            pltpu.VMEM((MEM * ROWS, LEV, LON), f32),
            pltpu.VMEM((3 * NSTEP, LEV, LANES), f32),
            pltpu.VMEM((2 * VAR, NGRP, LEV, LANES), f32),
            pltpu.VMEM((2 * VAR, NGRP, LEV, LANES), f32),
            pltpu.VMEM((2 * VAR, NGRP, LEV, LANES), f32),
            dma((6,)),
            dma((2,)),
            dma((2,)),
            dma((2,)),
            dma((2,)),
            dma((2,)),
            dma((2,)),
            dma((4,)),
            dma((4,)),
            dma((4,)),
            dma((4,)),
            dma((4,)),
            dma((4,)),
        ],
        compiler_params=pltpu.CompilerParams(
            collective_id=0, has_side_effects=True, vmem_limit_bytes=48 * 1024 * 1024
        ),
    )(
        pin(diff_rate),
        pin(step_counts),
        pin(pert),
        pin(tiles_of(control)),
        pin(tiles_of(departures)),
        pin(tiles_of(obs_weight)),
    )
    return (from_tiles(inc, (LEV, VAR, ROWS, LON)), from_tiles(grad, (MEM, LEV, ROWS, LON)))


def solution(mesh):
    in_specs = (
        P("grp", None, None, "dom", None),
        P("grp", None, "dom", None),
        P(None, None, "dom", None),
        P(None, None, "dom", None),
        P(),
        P(),
    )
    out_specs = (P(None, None, "dom", None), P("grp", None, "dom", None))
    return jax.shard_map(
        per_device, mesh=mesh, in_specs=in_specs, out_specs=out_specs, check_vma=False
    )
```

```python
import functools
import math

import jax
import jax.numpy as jnp
from jax import lax
from jax.experimental import pallas as pl
from jax.experimental.pallas import tpu as pltpu
from jax.sharding import PartitionSpec as P

NSTEP = 4
MEM = 2
LEV = 8
VAR = 2
ROWS = 4
LON = 1024
LANES = 128
TILES = LON // LANES
SLOT = 16
HALF = LON // 2
NDOM = 64
NGRP = 16
MESH = pl.DeviceIdType.MESH
FAR_FIRST_8 = (4, 3, 5, 2, 6, 1, 7)
FAR_FIRST_16 = (8, 7, 9, 6, 10, 5, 11, 4, 12, 3, 13, 2, 14, 1, 15)


def lane_iota(shape):
    return lax.broadcasted_iota(jnp.int32, shape, len(shape) - 1)


def remote(src, dst, send_sem, recv_sem, device):
    return pltpu.make_async_remote_copy(
        src_ref=src,
        dst_ref=dst,
        send_sem=send_sem,
        recv_sem=recv_sem,
        device_id=device,
        device_id_type=MESH,
    )


def wait_bytes(ref, sem):
    pltpu.make_async_copy(ref, ref, sem).wait()


def wide(tile):
    return jnp.concatenate([tile] * TILES, axis=1)


def sweeps(src, other, coef, m, emit):
    bufs = (src, other)
    for s in range(NSTEP):
        old, new = bufs[s % 2], bufs[(s + 1) % 2]
        first, last = s + 1, 3 * ROWS - 1 - s
        north = old[m, first - 1]
        here = old[m, first]
        for row in range(first, last):
            south = old[m, row + 1]
            which = 0 if ROWS <= row < 2 * ROWS else (1 if row < ROWS else 2)
            rate = wide(coef[3 * s + which])
            lap = (
                north
                + south
                + pltpu.roll(here, 1, axis=1)
                + pltpu.roll(here, LON - 1, axis=1)
                - 4.0 * here
            )
            value = here + rate * lap
            if s == NSTEP - 1:
                emit(row - ROWS, value)
            else:
                new[m, row] = value
            north, here = here, south


def kernel(
    factor,
    rate_hbm,
    steps_hbm,
    pert_hbm,
    ctl_hbm,
    dep_hbm,
    wgt_hbm,
    inc_ref,
    grad_ref,
    rate_ref,
    steps_ref,
    pert_ref,
    ctl_ref,
    dep_ref,
    wgt_ref,
    pf,
    packed,
    mid,
    got,
    pert,
    ext,
    own16,
    up16,
    dn16,
    tmp,
    ext2,
    own16b,
    up16b,
    dn16b,
    loc,
    coef,
    part,
    red,
    incs,
    load_sem,
    one_send,
    one_recv,
    two_send,
    two_recv,
    halo_send,
    halo_recv,
    rs_send,
    rs_recv,
    ag_send,
    ag_recv,
    adj_send,
    adj_recv,
):
    loads = [
        pltpu.make_async_copy(src, dst, load_sem.at[n])
        for n, (src, dst) in enumerate(
            (
                (pert_hbm, pert_ref),
                (ctl_hbm, ctl_ref),
                (dep_hbm, dep_ref),
                (wgt_hbm, wgt_ref),
                (rate_hbm, rate_ref),
                (steps_hbm, steps_ref),
            )
        )
    ]
    for load in loads:
        load.start()

    g = lax.axis_index("grp")
    d = lax.axis_index("dom")
    y, c = d // TILES, lax.rem(d, TILES)
    below = lax.rem(d + 1, NDOM)
    above = lax.rem(d + NDOM - 1, NDOM)

    barrier = pltpu.get_barrier_semaphore()

    def greet(to):
        pl.semaphore_signal(barrier, inc=1, device_id=to, device_id_type=MESH)

    def y_mate(k):
        return lax.rem(y + k, TILES)

    def z_mate(k):
        return lax.rem(c + k, TILES)

    for k in FAR_FIRST_8:
        greet((g, y_mate(k) * TILES + c))
        greet((g, y * TILES + z_mate(k)))
    for k in FAR_FIRST_16:
        greet((lax.rem(g + k, NGRP), d))

    @pl.when(c == TILES - 1)
    def _():
        greet((g, below))

    @pl.when(c == 0)
    def _():
        greet((g, above))

    loads[0].wait()
    pf[...] = pert_ref[...].astype(jnp.float32)
    low = lane_iota((LEV, LANES)) < 64
    for v in range(VAR):

        def pack(q, carry):
            a = pf[pl.ds(q * 2 + v, LEV, stride=64), :]
            b = pf[pl.ds(512 + q * 2 + v, LEV, stride=64), :]
            first = jnp.where(low, a, pltpu.roll(b, 64, axis=1))
            second = jnp.where(low, pltpu.roll(a, 64, axis=1), b)
            to_y, to_c = q // 4, 2 * lax.rem(q, 4)
            packed[v, to_y, to_c] = first.astype(jnp.bfloat16)
            packed[v, to_y, to_c + 1] = second.astype(jnp.bfloat16)
            return carry

        lax.fori_loop(0, NDOM // 2, pack, 0, unroll=4)

    loads[1].wait()
    ends = c // (TILES - 1) + (TILES - 1 - c) // (TILES - 1)
    pl.semaphore_wait(barrier, 2 * (TILES - 1) + NGRP - 1 + ends)

    def first_stage(v, k):
        if v == 0:
            to = y_mate(k)
            src, dst, device = packed.at[v, to], mid.at[v, y], (g, to * TILES + c)
        else:
            to = z_mate(k)
            src, dst, device = packed.at[v, :, to], mid.at[v, :, c], (g, y * TILES + to)
        remote(src, dst, one_send.at[v], one_recv.at[v], device).start()

    def second_stage(v, k):
        if v == 0:
            to = z_mate(k)
            src, dst, device = mid.at[v, :, to], got.at[v, :, c], (g, y * TILES + to)
        else:
            to = y_mate(k)
            src, dst, device = mid.at[v, to], got.at[v, y], (g, to * TILES + c)
        remote(src, dst, two_send.at[v], two_recv.at[v], device).start()

    def forward(v):
        wait_bytes(mid.at[v, pl.ds(0, TILES - 1)], one_recv.at[v])
        for k in FAR_FIRST_8:
            second_stage(v, k)
        if v == 0:
            got[v, :, c] = mid[v, :, c]
        else:
            got[v, y] = mid[v, y]

    for k in FAR_FIRST_8:
        for v in range(VAR):
            first_stage(v, k)
    mid[0, y] = packed[0, y]
    mid[1, :, c] = packed[1, :, c]
    def fill(n, carry):
        m, i = n // ROWS, lax.rem(n, ROWS)
        for t in range(TILES):
            cols = slice(t * LANES, (t + 1) * LANES)
            tile = ctl_ref[pl.ds(m * 256 + t * ROWS + i, LEV, stride=32), :]
            ext[m, ROWS + i, :, cols] = tile
            own16[m, i, :, cols] = tile.astype(jnp.bfloat16)
        return carry

    lax.fori_loop(0, MEM * ROWS, fill, 0)
    loads[4].wait()
    loads[5].wait()

    level = lax.broadcasted_iota(jnp.int32, (LEV, LANES), 0)
    rate = jnp.zeros((LEV, LANES), jnp.float32)
    count = jnp.zeros((LEV, LANES), jnp.int32)
    for l in range(LEV):
        rate = jnp.where(level == l, rate_ref[l], rate)
        count = jnp.where(level == l, steps_ref[l], count)
    has_up = jnp.where(d > 0, 1.0, 0.0).astype(jnp.float32)
    has_dn = jnp.where(d < NDOM - 1, 1.0, 0.0).astype(jnp.float32)
    for s in range(NSTEP):
        now = jnp.where(s < count, rate, 0.0)
        coef[3 * s] = now
        coef[3 * s + 1] = now * has_up
        coef[3 * s + 2] = now * has_dn

    def clear(buffer, base_row):
        for m in range(MEM):
            for i in range(ROWS):
                buffer[m, base_row + i] = jnp.zeros((LEV, LON), jnp.float32)

    def halo(field, mine, up, dn, cols, send, recv):
        pairs = (
            (field.at[:, pl.ds(6, 2), :, cols], field.at[:, pl.ds(2, 2), :, cols], below),
            (field.at[:, pl.ds(4, 2), :, cols], field.at[:, pl.ds(8, 2), :, cols], above),
            (mine.at[:, pl.ds(0, 2), :, cols], up.at[:, :, :, cols], below),
            (mine.at[:, pl.ds(2, 2), :, cols], dn.at[:, :, :, cols], above),
        )
        copies = [
            remote(src, dst, send.at[n], recv.at[n], (g, to))
            for n, (src, dst, to) in enumerate(pairs)
        ]
        for copy in copies:
            copy.start()
        return copies

    def widen(field, up, dn):
        for m in range(MEM):
            for i in range(2):
                field[m, i] = up[m, i].astype(jnp.float32)
                field[m, 10 + i] = dn[m, i].astype(jnp.float32)

    everything = pl.ds(0, LON)
    copies = halo(ext, own16, up16, dn16, everything, halo_send, halo_recv)
    forward(0)
    forward(1)

    for copy in copies:
        copy.wait()
    widen(ext, up16, dn16)

    @pl.when(d == 0)
    def _():
        clear(ext, 0)

    @pl.when(d == NDOM - 1)
    def _():
        clear(ext, 2 * ROWS)

    def localize(m, carry):
        def emit(i, value):
            loc[m * ROWS + i] = value

        sweeps(ext, tmp, coef, m, emit)
        return carry

    lax.fori_loop(0, MEM, localize, 0)

    slot = lane_iota((LEV, LANES)) // SLOT
    masks = {step: (slot & step) != 0 for step in (4, 2, 1)}

    for v in range(VAR):
        wait_bytes(got.at[v, pl.ds(0, TILES - 1)], two_recv.at[v])

        def relayout(t, carry):
            tiles = [got[v, t, n].astype(jnp.float32) for n in range(TILES)]
            for step in (4, 2, 1):
                high = masks[step]
                for a in range(TILES):
                    if a & step:
                        continue
                    p, q = tiles[a], tiles[a + step]
                    tiles[a] = jnp.where(high, pltpu.roll(q, step * SLOT, axis=1), p)
                    tiles[a + step] = jnp.where(
                        high, q, pltpu.roll(p, LANES - step * SLOT, axis=1)
                    )
            for k in range(TILES):
                pert[v, t, k] = tiles[k]
            cols = pl.ds(pl.multiple_of(t * LANES, LANES), LANES)
            for i in range(ROWS):
                part[2 * v + t // 4, 4 * i + lax.rem(t, 4)] = (
                    tiles[i] * loc[i, :, cols] + tiles[ROWS + i] * loc[ROWS + i, :, cols]
                )
            return carry

        lax.fori_loop(0, TILES, relayout, 0, unroll=2)
        for q in (2 * v, 2 * v + 1):
            for k in FAR_FIRST_16:
                to = lax.rem(g + k, NGRP)
                remote(
                    part.at[q, to], red.at[q, g], rs_send.at[q], rs_recv.at[q], (to, d)
                ).start()
            red[q, g] = part[q, g]

    for q in range(2 * VAR):
        wait_bytes(red.at[q, pl.ds(0, NGRP - 1)], rs_recv.at[q])
        total = red[q, 0]
        for n in range(1, NGRP):
            total = total + red[q, n]
        incs[q, g] = total * factor
        for k in FAR_FIRST_16:
            remote(
                incs.at[q, g],
                incs.at[q, g],
                ag_send.at[q],
                ag_recv.at[q],
                (lax.rem(g + k, NGRP), d),
            ).start()

    loads[2].wait()
    loads[3].wait()
    copies = []
    for h in range(2):
        for v in range(VAR):
            wait_bytes(incs.at[2 * v + h, pl.ds(0, NGRP - 1)], ag_recv.at[2 * v + h])

        def back(i, carry):
            for n in range(TILES // 2):
                t = h * (TILES // 2) + n
                cols = slice(t * LANES, (t + 1) * LANES)
                res = []
                for v in range(VAR):
                    lines = pl.ds(v * 32 + t * ROWS + i, LEV, stride=64)
                    inc = incs[2 * v + h, 4 * i + n]
                    inc_ref[lines, :] = inc
                    res.append(wgt_ref[lines, :] * (inc - dep_ref[lines, :]))
                for m in range(MEM):
                    adj = (
                        pert[0, t, m * ROWS + i] * res[0] + pert[1, t, m * ROWS + i] * res[1]
                    ) * factor
                    ext2[m, ROWS + i, :, cols] = adj
                    own16b[m, i, :, cols] = adj.astype(jnp.bfloat16)
            return carry

        lax.fori_loop(0, ROWS, back, 0)
        cols = pl.ds(h * HALF, HALF)
        copies += halo(
            ext2, own16b, up16b, dn16b, cols, adj_send.at[pl.ds(4 * h, 4)], adj_recv.at[pl.ds(4 * h, 4)]
        )

    for v in range(VAR):
        wait_bytes(packed.at[v, pl.ds(0, TILES - 1)], one_send.at[v])
        wait_bytes(mid.at[v, pl.ds(0, TILES - 1)], two_send.at[v])
    for q in range(2 * VAR):
        wait_bytes(part.at[q, pl.ds(0, NGRP - 1)], rs_send.at[q])
        wait_bytes(incs.at[q, pl.ds(0, NGRP - 1)], ag_send.at[q])
    for copy in copies:
        copy.wait()
    widen(ext2, up16b, dn16b)

    @pl.when(d == 0)
    def _():
        clear(ext2, 0)

    @pl.when(d == NDOM - 1)
    def _():
        clear(ext2, 2 * ROWS)

    def gradient(m, carry):
        def emit(i, value):
            for t in range(TILES):
                lines = pl.ds(m * 256 + t * ROWS + i, LEV, stride=32)
                grad_ref[lines, :] = ctl_ref[lines, :] + value[:, t * LANES : (t + 1) * LANES]

        sweeps(ext2, tmp, coef, m, emit)
        return carry

    lax.fori_loop(0, MEM, gradient, 0)


def tiles_of(x):
    a, b, rows, lon = x.shape
    return (
        x.reshape(a, b, rows, lon // LANES, LANES)
        .transpose(0, 1, 3, 2, 4)
        .reshape(a * b * rows * lon // LANES, LANES)
    )


def from_tiles(x, shape):
    a, b, rows, lon = shape
    return (
        x.reshape(a, b, lon // LANES, rows, LANES).transpose(0, 1, 3, 2, 4).reshape(shape)
    )


def pin(x):
    return pltpu.with_memory_space_constraint(x, pltpu.HBM)


def per_device(pert_fcst, control, departures, obs_weight, diff_rate, step_counts):
    members = MEM * lax.axis_size("grp")
    factor = 1.0 / math.sqrt(members - 1)
    pert = (
        pert_fcst.reshape(MEM, LEV, VAR, 32, LANES)
        .transpose(0, 1, 3, 2, 4)
        .reshape(MEM * LEV * 32 * VAR, LANES)
    )
    vmem = pl.BlockSpec(memory_space=pltpu.VMEM)
    flat = (MEM * LEV * ROWS * TILES, LANES)
    f32, bf16 = jnp.float32, jnp.bfloat16
    hbm = pl.BlockSpec(memory_space=pltpu.HBM)
    dma = pltpu.SemaphoreType.DMA
    inc, grad = pl.pallas_call(
        functools.partial(kernel, factor),
        out_shape=(jax.ShapeDtypeStruct(flat, f32), jax.ShapeDtypeStruct(flat, f32)),
        in_specs=[hbm] * 6,
        out_specs=(vmem, vmem),
        scratch_shapes=[
            pltpu.SMEM((LEV,), f32),
            pltpu.SMEM((LEV,), jnp.int32),
            pltpu.VMEM((1024, LANES), bf16),
            pltpu.VMEM(flat, f32),
            pltpu.VMEM(flat, f32),
            pltpu.VMEM(flat, f32),
            pltpu.VMEM((1024, LANES), f32),
            pltpu.VMEM((VAR, TILES, TILES, LEV, LANES), bf16),
            pltpu.VMEM((VAR, TILES, TILES, LEV, LANES), bf16),
            pltpu.VMEM((VAR, TILES, TILES, LEV, LANES), bf16),
            pltpu.VMEM((VAR, TILES, MEM * ROWS, LEV, LANES), f32),
            pltpu.VMEM((MEM, 3 * ROWS, LEV, LON), f32),
            pltpu.VMEM((MEM, ROWS, LEV, LON), bf16),
            pltpu.VMEM((MEM, 2, LEV, LON), bf16),
            pltpu.VMEM((MEM, 2, LEV, LON), bf16),
            pltpu.VMEM((MEM, 3 * ROWS, LEV, LON), f32),
            pltpu.VMEM((MEM, 3 * ROWS, LEV, LON), f32),
            pltpu.VMEM((MEM, ROWS, LEV, LON), bf16),
            pltpu.VMEM((MEM, 2, LEV, LON), bf16),
            pltpu.VMEM((MEM, 2, LEV, LON), bf16),
            pltpu.VMEM((MEM * ROWS, LEV, LON), f32),
            pltpu.VMEM((3 * NSTEP, LEV, LANES), f32),
            pltpu.VMEM((2 * VAR, NGRP, LEV, LANES), f32),
            pltpu.VMEM((2 * VAR, NGRP, LEV, LANES), f32),
            pltpu.VMEM((2 * VAR, NGRP, LEV, LANES), f32),
            dma((6,)),
            dma((2,)),
            dma((2,)),
            dma((2,)),
            dma((2,)),
            dma((4,)),
            dma((4,)),
            dma((4,)),
            dma((4,)),
            dma((4,)),
            dma((4,)),
            dma((8,)),
            dma((8,)),
        ],
        compiler_params=pltpu.CompilerParams(
            collective_id=0, has_side_effects=True, vmem_limit_bytes=48 * 1024 * 1024
        ),
    )(
        pin(diff_rate),
        pin(step_counts),
        pin(pert),
        pin(tiles_of(control)),
        pin(tiles_of(departures)),
        pin(tiles_of(obs_weight)),
    )
    return (from_tiles(inc, (LEV, VAR, ROWS, LON)), from_tiles(grad, (MEM, LEV, ROWS, LON)))


def solution(mesh):
    in_specs = (
        P("grp", None, None, "dom", None),
        P("grp", None, "dom", None),
        P(None, None, "dom", None),
        P(None, None, "dom", None),
        P(),
        P(),
    )
    out_specs = (P(None, None, "dom", None), P("grp", None, "dom", None))
    return jax.shard_map(
        per_device, mesh=mesh, in_specs=in_specs, out_specs=out_specs, check_vma=False
    )
```
